32 devices in a mesh: dp: 4 (over y, x), section: 2 (over core), ctx: 4 (over z).
Axes of the slice: x: 2, y: 2, z: 4, core: 2. Of those that a mesh axis runs over, the one named last changes fastest.
Arguments:
- queries: bfloat16 [4, 2, 512, 2048], P('dp', 'section', 'ctx'), may hold values from -6 to 6
- key_rows: bfloat16 [4, 2, 512, 128], P('dp', 'section', 'ctx'), may hold values from -6 to 6
- value_rows: bfloat16 [4, 2, 512, 128], P('dp', 'section', 'ctx'), may hold values from -6 to 6
- out_grad: bfloat16 [4, 2, 512, 2048], P('dp', 'section', 'ctx'), may hold values from -6 to 6
- attn_out: bfloat16 [4, 2, 512, 2048], P('dp', 'section', 'ctx'), may hold values from -1.796875 to 1.796875
- log_norm: float32 [4, 2, 512, 16], P('dp', 'section', 'ctx'), may hold values from 2 to 5
- selected: int32 [4, 2, 8, 16], P('dp', 'section', 'ctx'), may hold values from -1 to 7, as said below
- gate_weight: float32 [2, 16, 128], P('section'), may hold values from -0.5 to 0.5
- gate_bias: float32 [2, 16], P('section'), may hold values from -2 to 2
Outputs:
- query_grad_prev: bfloat16 [4, 2, 512, 2048], P('dp', 'section', 'ctx')
- key_grad_prev: bfloat16 [4, 2, 512, 128], P('dp', 'section', 'ctx')
- value_grad_prev: bfloat16 [4, 2, 512, 128], P('dp', 'section', 'ctx')
- gate_weight_grad: float32 [2, 16, 128], P('section')
- gate_bias_grad: float32 [2, 16], P('section')
The draws below stay inside these ranges and needn't reach their ends.
Inputs may be any that keep to these rules, and one draw needn't show every extreme that they name: `selected`: each row of block b lists distinct blocks of 0 to b, always b itself and block 0, min(16, b + 1) of them, followed by -1 entries.
All inputs are finite; a program needn't handle non-finite values.
Results may differ from the reference program's by a relative error of at most 0.013.
Values may be sent and summed in bfloat16 or wider, within the bound.
No kernel may reach another device: no remote copies, remote signals or barrier semaphores. Data moves between devices by JAX's collectives and lax.ppermute only.
A program may use at most 64 MiB of HBM per device.

```python
import jax
import jax.numpy as jnp
from jax import lax

H = 16
DH = 128
BLK = 64
SEL = 16
L = 512
NB = 8
N_DP = 4
N_SECTION = 2


def draw_selected(key, part):
    width = NB + SEL
    count = N_DP * N_SECTION * NB
    row_keys = jax.random.split(key, count)
    ranks = jax.vmap(lambda one_key: jax.random.permutation(one_key, width))(row_keys).astype(jnp.int32)
    ranks = ranks.reshape(N_DP, N_SECTION, NB, width)
    column = jnp.arange(width, dtype=jnp.int32)[None, None, None, :]
    block = jnp.arange(NB, dtype=jnp.int32)[None, None, :, None]
    scores = jnp.where(column <= block, ranks + 2, -1 - column)
    scores = jnp.where(column == block, width + 3, scores)
    scores = jnp.where(column == 0, width + 4, scores)
    values, indices = lax.top_k(scores, SEL)
    return jnp.where(values >= 0, indices, -1).astype(jnp.int32)


def steps_of(key, dims, cuts, low, top_value):
    def one(axis_at, blocks):
        steps = jax.random.uniform(jax.random.fold_in(jax.random.fold_in(key, 6), axis_at), (blocks,), jnp.float32, low / len(cuts), top_value / len(cuts))
        return jnp.repeat(jnp.exp(steps), dims[axis_at] // blocks).reshape((-1,) + (1,) * (len(dims) - axis_at - 1))

    gain = one(*cuts[0])
    for cut in cuts[1:]:
        gain = gain * one(*cut)
    return gain


def scatter_about(stream_key, extent, scale, limit, cuts=(), held_as=jnp.bfloat16):
    values = scale * jax.random.normal(stream_key, extent, jnp.float32)
    if cuts:
        values = values * steps_of(stream_key, extent, cuts, -0.22, 0.18)
    return jnp.clip(values, -limit, limit).astype(held_as)


def setup_inputs(seed: int = 0) -> dict:
    key_list = jax.random.split(jax.random.key(seed), 10)
    return {
        "queries": scatter_about(key_list[0], (N_DP, N_SECTION, L, H * DH), 1.0, 6.0, ((0, 4), (1, 2), (2, 4))),
        "key_rows": scatter_about(key_list[1], (N_DP, N_SECTION, L, DH), 1.0, 6.0, ((0, 4), (1, 2), (2, 4))),
        "value_rows": scatter_about(key_list[2], (N_DP, N_SECTION, L, DH), 1.0, 6.0, ((0, 4), (1, 2), (2, 4))),
        "out_grad": scatter_about(key_list[3], (N_DP, N_SECTION, L, H * DH), 1.0, 6.0, ((0, 4), (1, 2), (2, 4))),
        "attn_out": scatter_about(key_list[4], (N_DP, N_SECTION, L, H * DH), 0.3, 1.796875, ((0, 4), (1, 2), (2, 4))),
        "log_norm": jnp.clip(2.0 + 3.0 * jax.random.uniform(key_list[5], (N_DP, N_SECTION, L, H), jnp.float32) ** steps_of(key_list[5], (N_DP, N_SECTION, L, H), ((0, 4), (1, 2), (2, 4)), -0.2, 0.2), 2.0, 5.0),
        "selected": draw_selected(jax.random.fold_in(key_list[9], 71), 0),
        "gate_weight": scatter_about(key_list[7], (N_SECTION, H, DH), DH ** -0.5, 0.5, ((0, 2),), jnp.float32),
        "gate_bias": jnp.clip(jax.random.uniform(key_list[8], (N_SECTION, H), jnp.float32, -2.0, 2.0) * steps_of(key_list[8], (N_SECTION, H), ((0, 2),), -0.4, 0.0), -2.0, 2.0),
    }


def pair_grads(inputs):
    queries, key_rows, value_rows, out_grad, attn_out, log_norm, chosen, weight, bias = inputs
    seq_len = queries.shape[0]
    query3 = queries.reshape(seq_len, H, DH).astype(jnp.float32)
    gate = jax.nn.sigmoid(jnp.sum(query3 * weight[None], axis=-1) + bias[None])
    grad3 = out_grad.reshape(seq_len, H, DH).astype(jnp.float32)
    output3 = attn_out.reshape(seq_len, H, DH).astype(jnp.float32)
    branch_grad = (gate[:, :, None] * grad3).astype(jnp.bfloat16)
    row_delta = jnp.sum(branch_grad.astype(jnp.float32) * output3, axis=-1)
    pre_grad = jnp.sum(grad3 * output3, axis=-1) * gate * (1.0 - gate)
    weight_grad = jnp.sum(pre_grad[:, :, None] * query3, axis=0)
    bias_grad = jnp.sum(pre_grad, axis=0)
    factor = DH ** -0.5
    query_flat = queries.reshape(seq_len * H, DH)
    grad_flat = branch_grad.reshape(seq_len * H, DH)
    delta_flat = row_delta.reshape(-1)
    norm_flat = log_norm.reshape(-1)
    pre_flat = pre_grad.reshape(-1)
    key_blocks = key_rows.reshape(NB, BLK, DH)
    value_blocks = value_rows.reshape(NB, BLK, DH)
    weight_tile = jnp.tile(weight, (BLK, 1))

    def step(state, block):
        key_acc, value_acc = state
        first = (block * BLK * H).astype(jnp.int32)
        query_blk = lax.dynamic_slice_in_dim(query_flat, first, BLK * H, 0)
        grad_blk = lax.dynamic_slice_in_dim(grad_flat, first, BLK * H, 0)
        delta_blk = lax.dynamic_slice_in_dim(delta_flat, first, BLK * H, 0)
        norm_blk = lax.dynamic_slice_in_dim(norm_flat, first, BLK * H, 0)
        pre_blk = lax.dynamic_slice_in_dim(pre_flat, first, BLK * H, 0)
        row_pos = block * BLK + jnp.arange(BLK * H, dtype=jnp.int32) // H
        ids = chosen[block]
        safe = jnp.maximum(ids, 0).astype(jnp.int32)
        key_sel = key_blocks[safe].reshape(SEL * BLK, DH)
        value_sel = value_blocks[safe].reshape(SEL * BLK, DH)
        key_pos = (safe[:, None] * BLK + jnp.arange(BLK, dtype=jnp.int32)[None, :]).reshape(-1)
        usable = jnp.repeat(ids >= 0, BLK)
        allowed = usable[None, :] & (key_pos[None, :] <= row_pos[:, None])
        scores = jnp.dot(query_blk, key_sel.T, preferred_element_type=jnp.float32) * factor
        probs = jnp.where(allowed, jnp.exp(jnp.where(allowed, scores - norm_blk[:, None], 0.0)), 0.0)
        probs_b = probs.astype(jnp.bfloat16)
        dprobs = jnp.dot(grad_blk, value_sel.T, preferred_element_type=jnp.float32)
        dscores = (probs * (dprobs - delta_blk[:, None])).astype(jnp.bfloat16)
        query_grad = factor * jnp.dot(dscores, key_sel, preferred_element_type=jnp.float32) + pre_blk[:, None] * weight_tile
        key_part = factor * jnp.dot(dscores.T, query_blk, preferred_element_type=jnp.float32)
        value_part = jnp.dot(probs_b.T, grad_blk, preferred_element_type=jnp.float32)
        key_acc = key_acc.at[safe].add(key_part.reshape(SEL, BLK * DH))
        value_acc = value_acc.at[safe].add(value_part.reshape(SEL, BLK * DH))
        return (key_acc, value_acc), query_grad.astype(jnp.bfloat16)

    zeros_kv = jnp.zeros((NB, BLK * DH), jnp.float32)
    (key_acc, value_acc), query_blocks = lax.scan(step, (zeros_kv, zeros_kv), jnp.arange(NB, dtype=jnp.int32))
    query_grad = query_blocks.reshape(seq_len, H * DH)
    key_out = key_acc.reshape(seq_len, DH).astype(jnp.bfloat16)
    value_out = value_acc.reshape(seq_len, DH).astype(jnp.bfloat16)
    return query_grad, key_out, value_out, weight_grad, bias_grad


def flatten_pairs(array):
    return array.reshape((N_DP * N_SECTION,) + array.shape[2:])


def shift_section(array):
    return jnp.concatenate([array[:, 1:], jnp.zeros_like(array[:, :1])], axis=1)


def reference(queries, key_rows, value_rows, out_grad, attn_out, log_norm, selected, gate_weight, gate_bias):
    weight_rep = jnp.broadcast_to(gate_weight[None], (N_DP, N_SECTION, H, DH))
    bias_rep = jnp.broadcast_to(gate_bias[None], (N_DP, N_SECTION, H))
    inputs = tuple(flatten_pairs(item) for item in (queries, key_rows, value_rows, out_grad, attn_out, log_norm, selected, weight_rep, bias_rep))
    query_grad, key_grad, value_grad, weight_grad, bias_grad = lax.map(pair_grads, inputs)
    query_grad = query_grad.reshape(N_DP, N_SECTION, L, H * DH)
    key_grad = key_grad.reshape(N_DP, N_SECTION, L, DH)
    value_grad = value_grad.reshape(N_DP, N_SECTION, L, DH)
    weight_total = jnp.sum(weight_grad.reshape(N_DP, N_SECTION, H, DH), axis=0)
    bias_total = jnp.sum(bias_grad.reshape(N_DP, N_SECTION, H), axis=0)
    return (shift_section(query_grad), shift_section(key_grad), shift_section(value_grad), weight_total, bias_total)
```

```python
import functools

import jax
import jax.numpy as jnp
from jax import lax
from jax.experimental import pallas as pl
from jax.experimental.pallas import tpu as pltpu
from jax.sharding import PartitionSpec as P

BLK = 64
OUT = 1e30
LOG2E = 1.4426950408889634
NT = (((1,), (1,)), ((), ()))
TN = (((0,), (0,)), ((), ()))
VMEM_BYTES = 48 * 1024 * 1024


def dot32(a, b, dims=(((1,), (0,)), ((), ())), precision=None):
    return lax.dot_general(a, b, dims, precision=precision, preferred_element_type=jnp.float32)


def split16(x):
    high = x.astype(jnp.bfloat16)
    low = (x - high.astype(jnp.float32)).astype(jnp.bfloat16)
    return high, low


def head_blocks(weight):
    heads = weight.shape[0]
    row = lax.broadcasted_iota(jnp.int32, weight.shape, 0)
    return jnp.concatenate([jnp.where(row == h, weight, 0.0) for h in range(heads)], axis=1)


def stats_kernel(query, grad, output, norm, weight, bias, stats, partial):
    heads, head_dim = weight.shape
    length = query.shape[0]
    eye = (
        lax.broadcasted_iota(jnp.int32, (heads, heads), 0)
        == lax.broadcasted_iota(jnp.int32, (heads, heads), 1)
    ).astype(jnp.float32)
    exact = lax.Precision.HIGHEST
    norm_rows = dot32(eye, norm[...], NT, exact)
    bias_col = jnp.sum(eye * bias[...], axis=1, keepdims=True)
    weight_high, weight_low = split16(head_blocks(weight[...]))
    both = dot32(jnp.concatenate([weight_high, weight_low], axis=0), query[...], NT)
    logit = both[:heads] + both[heads:] + bias_col
    product = grad[...].astype(jnp.float32) * output[...].astype(jnp.float32)
    high, low = split16(product)
    ones = head_blocks(jnp.ones((heads, head_dim), jnp.float32)).astype(jnp.bfloat16)
    inner = dot32(ones, high, NT) + dot32(ones, low, NT)
    gate = jax.nn.sigmoid(logit)
    softplus = jnp.maximum(-logit, 0.0) + jnp.log1p(jnp.exp(-jnp.abs(logit)))
    pre_grad = inner * gate * (1.0 - gate)
    stats[0:heads] = LOG2E * (norm_rows + softplus)
    stats[heads : 2 * heads] = inner
    stats[2 * heads : 3 * heads] = pre_grad
    pre_high, pre_low = split16(pre_grad)
    wide = dot32(jnp.concatenate([pre_high, pre_low], axis=0), query[...])
    wide = wide[:heads] + wide[heads:]
    for h in range(heads):
        partial[h : h + 1, :] = wide[h : h + 1, h * head_dim : (h + 1) * head_dim]
    total = jnp.sum(pre_grad, axis=1, keepdims=True)
    lane = lax.broadcasted_iota(jnp.int32, (heads, head_dim), 1)
    row = lax.broadcasted_iota(jnp.int32, (heads, head_dim), 0)
    partial[heads : heads + 8, :] = jnp.broadcast_to(
        jnp.sum(jnp.where(lane == row, total, 0.0), axis=0, keepdims=True), (8, head_dim)
    )


def attention_kernel(count, *refs):
    query, grad, stats, chosen, weight = refs[:5]
    kv = refs[5 : 5 + count]
    query_grad = refs[5 + count]
    kv_grad = refs[6 + count :]
    heads, head_dim = weight.shape
    length = query.shape[0]
    local = length // BLK
    factor = head_dim ** (-0.5)
    rank = lax.axis_index("ctx")
    section = lax.axis_index("section")
    pair = 2 * length
    lane = lax.broadcasted_iota(jnp.int32, (1, length), 1)

    @pl.when(section == 0)
    def _():
        query_grad[...] = jnp.zeros_like(query_grad)
        for ref in kv_grad:
            ref[...] = jnp.zeros_like(ref)

    @pl.when(section > 0)
    def _():
        listed = chosen[...]
        keys = jnp.concatenate([ref[:, :head_dim] for ref in kv], axis=0)
        values = jnp.concatenate([ref[:, head_dim:] for ref in kv], axis=0)
        keys_t = keys.T
        outs = []
        for d in range(count):
            for b in range(local):
                block = lax.rem(rank - d + count, count) * local + b
                hit = jnp.max(jnp.where(listed == block, 1.0, 0.0), axis=1, keepdims=True)
                one = jnp.zeros((1, length), jnp.float32)
                for at in range(local):
                    one = jnp.where(lane // BLK == at, (1.0 - hit[at : at + 1]) * OUT, one)
                outs.append(jnp.broadcast_to(one, (BLK, length)))
        later = lax.broadcasted_iota(jnp.int32, (length, length), 0) > lax.broadcasted_iota(
            jnp.int32, (length, length), 1
        )
        own = jnp.where(later, OUT, jnp.concatenate(outs[:local], axis=0))
        masked = jnp.concatenate([own] + outs[local:], axis=0)
        masked = jnp.concatenate([masked, masked], axis=1)
        weight_high, weight_low = split16(head_blocks(weight[...]))
        pre_high, pre_low = split16(stats[2 * heads : 3 * heads])
        gate_term = dot32(
            jnp.concatenate([pre_high, pre_low, pre_high], axis=0),
            jnp.concatenate([weight_high, weight_high, weight_low], axis=0),
            TN,
        )
        key_acc = jnp.zeros((count * length, head_dim), jnp.float32)
        value_acc = jnp.zeros((count * length, head_dim), jnp.float32)
        for h in range(0, heads, 2):
            first = slice(h * head_dim, (h + 1) * head_dim)
            second = slice((h + 1) * head_dim, (h + 2) * head_dim)
            query_p = jnp.concatenate([query[:, first], query[:, second]], axis=0)
            grad_p = jnp.concatenate([grad[:, first], grad[:, second]], axis=0)
            norm_p = jnp.concatenate([stats[h : h + 1], stats[h + 1 : h + 2]], axis=1)
            inner_p = jnp.concatenate(
                [stats[heads + h : heads + h + 1], stats[heads + h + 1 : heads + h + 2]], axis=1
            )
            scores = dot32(keys, query_p, NT)
            raw = dot32(values, grad_p, NT)
            probs = jnp.exp2(scores * (factor * LOG2E) - (masked + norm_p))
            dscores = (probs * (raw - inner_p)).astype(jnp.bfloat16)
            value_acc += dot32(probs.astype(jnp.bfloat16), grad_p)
            key_acc += dot32(dscores, query_p)
            turned = dot32(keys_t, dscores).T
            query_grad[:, first] = (factor * turned[:length] + gate_term[:, first]).astype(
                jnp.bfloat16
            )
            query_grad[:, second] = (factor * turned[length:] + gate_term[:, second]).astype(
                jnp.bfloat16
            )
        for d, ref in enumerate(kv_grad):
            rows = slice(d * length, (d + 1) * length)
            ref[:, :head_dim] = (factor * key_acc[rows]).astype(jnp.bfloat16)
            ref[:, head_dim:] = value_acc[rows].astype(jnp.bfloat16)


def total_over(array, axis):
    size = lax.axis_size(axis)
    parts = [
        lax.ppermute(array, axis, [(i, (i + d) % size) for i in range(size)])
        for d in range(1, size)
    ]
    return functools.reduce(jnp.add, parts, array)


def on_device(
    queries, key_rows, value_rows, out_grad, attn_out, log_norm, selected, gate_weight, gate_bias
):
    query = queries[0, 0]
    grad = out_grad[0, 0]
    weight = gate_weight[0]
    length, width = query.shape
    heads, head_dim = weight.shape
    size = lax.axis_size("ctx")
    sections = lax.axis_size("section")
    both_axes = ("section", "ctx")
    places = [(s, r) for s in range(sections) for r in range(size)]

    def place(s, r):
        return s * size + r

    own_kv = jnp.concatenate([key_rows[0, 0], value_rows[0, 0]], axis=1)
    kv = [own_kv]
    for d in range(1, size):
        route = [
            (place(s, r), place(s, (r + d) % size) if s else place(s, r)) for s, r in places
        ]
        kv.append(lax.ppermute(own_kv, both_axes, route))
    params = pltpu.CompilerParams(vmem_limit_bytes=VMEM_BYTES)
    stats, partial = pl.pallas_call(
        stats_kernel,
        out_shape=(
            jax.ShapeDtypeStruct((3 * heads, length), jnp.float32),
            jax.ShapeDtypeStruct((heads + 8, head_dim), jnp.float32),
        ),
        compiler_params=params,
        cost_estimate=pl.CostEstimate(
            flops=8 * heads * length * width, transcendentals=0, bytes_accessed=6 * length * width
        ),
        name="gate_stats",
    )(query, grad, attn_out[0, 0], log_norm[0, 0], weight, gate_bias)
    results = pl.pallas_call(
        functools.partial(attention_kernel, size),
        out_shape=(jax.ShapeDtypeStruct((length, width), jnp.bfloat16),)
        + (jax.ShapeDtypeStruct((length, 2 * head_dim), jnp.bfloat16),) * size,
        compiler_params=params,
        cost_estimate=pl.CostEstimate(
            flops=10 * size * length * length * width,
            transcendentals=size * length * length * heads,
            bytes_accessed=6 * length * width,
        ),
        name="attention_grads",
    )(query, grad, stats, selected[0, 0], weight, *kv)
    query_sent = lax.ppermute(
        results[0], "section", [(s, (s - 1) % sections) for s in range(sections)]
    )
    kv_sum = jnp.zeros((length, 2 * head_dim), jnp.float32)
    for d, part in enumerate(results[1:]):
        route = [
            (place(s, r), place(s - 1, (r - d) % size) if s else place(sections - 1, r))
            for s, r in places
        ]
        kv_sum += lax.ppermute(part, both_axes, route).astype(jnp.float32)
    kv_sent = kv_sum.astype(jnp.bfloat16)
    total = total_over(total_over(partial, "dp"), "ctx")
    return (
        query_sent[None, None],
        kv_sent[None, None, :, :head_dim],
        kv_sent[None, None, :, head_dim:],
        total[None, :heads],
        total[heads : heads + 1, :heads],
    )


def solution(mesh):
    rows = P("dp", "section", "ctx", None)
    return jax.shard_map(
        on_device,
        mesh=mesh,
        in_specs=(rows,) * 7 + (P("section", None, None), P("section", None)),
        out_specs=(rows,) * 3 + (P("section", None, None), P("section", None)),
        check_vma=False,
    )
```

```python
import functools

import jax
import jax.numpy as jnp
from jax import lax
from jax.experimental import pallas as pl
from jax.experimental.pallas import tpu as pltpu
from jax.sharding import PartitionSpec as P

BLK = 64
OUT = 1e30
LOG2E = 1.4426950408889634
NT = (((1,), (1,)), ((), ()))
TN = (((0,), (0,)), ((), ()))
VMEM_BYTES = 48 * 1024 * 1024


def dot32(a, b, dims=(((1,), (0,)), ((), ())), precision=None):
    return lax.dot_general(a, b, dims, precision=precision, preferred_element_type=jnp.float32)


def split16(x):
    high = x.astype(jnp.bfloat16)
    low = (x - high.astype(jnp.float32)).astype(jnp.bfloat16)
    return high, low


def head_blocks(weight):
    heads = weight.shape[0]
    row = lax.broadcasted_iota(jnp.int32, weight.shape, 0)
    return jnp.concatenate([jnp.where(row == h, weight, 0.0) for h in range(heads)], axis=1)


def pack_kernel(keys, values, packed, sems):
    length = keys.shape[0]
    copies = [
        pltpu.make_async_copy(keys, packed.at[:length], sems.at[0]),
        pltpu.make_async_copy(values, packed.at[length:], sems.at[1]),
    ]
    for copy in copies:
        copy.start()
    for copy in copies:
        copy.wait()


def stats_kernel(count, *refs):
    sources = refs[:7]
    query, grad, weight, stats, partial, output, norm, bias, chosen, sems = refs[7:]
    copies = [
        pltpu.make_async_copy(source, target, sems.at[i])
        for i, (source, target) in enumerate(
            zip(sources, (weight, norm, bias, chosen, query, grad, output), strict=True)
        )
    ]
    for copy in copies:
        copy.start()
    for copy in copies[:4]:
        copy.wait()
    heads, head_dim = weight.shape
    length = query.shape[0]
    local = length // BLK
    rank = lax.axis_index("ctx")
    listed = chosen[...]
    lane_block = lax.broadcasted_iota(jnp.int32, (1, length), 1) // BLK
    for d in range(count):
        for b in range(local):
            block = lax.rem(rank - d + count, count) * local + b
            hit = jnp.max(jnp.where(listed == block, 1.0, 0.0), axis=1, keepdims=True)
            one = jnp.zeros((1, length), jnp.float32)
            for at in range(local):
                one = jnp.where(lane_block == at, (1.0 - hit[at : at + 1]) * OUT, one)
            at = 3 * heads + d * local + b
            stats[at : at + 1] = one
    eye = (
        lax.broadcasted_iota(jnp.int32, (heads, heads), 0)
        == lax.broadcasted_iota(jnp.int32, (heads, heads), 1)
    ).astype(jnp.float32)
    bias_col = jnp.sum(eye * bias[...], axis=1, keepdims=True)
    weight_high, weight_low = split16(head_blocks(weight[...]))
    ones = head_blocks(jnp.ones((heads, head_dim), jnp.float32)).astype(jnp.bfloat16)
    copies[4].wait()
    both = dot32(jnp.concatenate([weight_high, weight_low], axis=0), query[...], NT)
    logit = both[:heads] + both[heads:] + bias_col
    gate = jax.nn.sigmoid(logit)
    softplus = jnp.maximum(-logit, 0.0) + jnp.log1p(jnp.exp(-jnp.abs(logit)))
    stats[0:heads] = LOG2E * (norm[...] + softplus)
    copies[5].wait()
    copies[6].wait()
    product = grad[...].astype(jnp.float32) * output[...].astype(jnp.float32)
    high, low = split16(product)
    inner = dot32(ones, high, NT) + dot32(ones, low, NT)
    pre_grad = inner * gate * (1.0 - gate)
    stats[heads : 2 * heads] = inner
    stats[2 * heads : 3 * heads] = pre_grad
    pre_high, pre_low = split16(pre_grad)
    wide = dot32(jnp.concatenate([pre_high, pre_low], axis=0), query[...])
    wide = wide[:heads] + wide[heads:]
    for h in range(heads):
        partial[h : h + 1, :] = wide[h : h + 1, h * head_dim : (h + 1) * head_dim]
    total = jnp.sum(pre_grad, axis=1, keepdims=True)
    lane = lax.broadcasted_iota(jnp.int32, (heads, head_dim), 1)
    row = lax.broadcasted_iota(jnp.int32, (heads, head_dim), 0)
    partial[heads : heads + 8, :] = jnp.broadcast_to(
        jnp.sum(jnp.where(lane == row, total, 0.0), axis=0, keepdims=True), (8, head_dim)
    )


def final_kernel(count, parts_count, *refs):
    kv = refs[:count]
    parts = refs[count : count + parts_count]
    key_grad, value_grad, weight_grad, bias_grad = refs[count + parts_count :]
    length = key_grad.shape[0]
    heads = weight_grad.shape[0]
    total = functools.reduce(jnp.add, [ref[...] for ref in parts])
    weight_grad[...] = total[:heads]
    bias_grad[...] = total[heads : heads + 1, :heads]
    total = functools.reduce(jnp.add, [ref[...].astype(jnp.float32) for ref in kv])
    total = total.astype(jnp.bfloat16)
    key_grad[...] = total[:length]
    value_grad[...] = total[length:]


def attention_kernel(count, *refs):
    query, grad, stats, weight = refs[:4]
    kv = refs[4 : 4 + count]
    query_grad = refs[4 + count]
    kv_grad = refs[5 + count :]
    heads, head_dim = weight.shape
    length = query.shape[0]
    local = length // BLK
    factor = head_dim ** (-0.5)
    section = lax.axis_index("section")

    @pl.when(section == 0)
    def _():
        query_grad[...] = jnp.zeros_like(query_grad)
        for ref in kv_grad:
            ref[...] = jnp.zeros_like(ref)

    @pl.when(section > 0)
    def _():
        keys = jnp.concatenate([ref[:length] for ref in kv], axis=0)
        values = jnp.concatenate([ref[length:] for ref in kv], axis=0)
        keys_t = keys.T
        outs = [
            jnp.broadcast_to(stats[3 * heads + i : 3 * heads + i + 1], (BLK, length))
            for i in range(count * local)
        ]
        later = lax.broadcasted_iota(jnp.int32, (length, length), 0) > lax.broadcasted_iota(
            jnp.int32, (length, length), 1
        )
        own = jnp.where(later, OUT, jnp.concatenate(outs[:local], axis=0))
        masked = jnp.concatenate([own] + outs[local:], axis=0)
        masked = jnp.concatenate([masked, masked], axis=1)
        weight_high, weight_low = split16(head_blocks(weight[...]))
        pre_high, pre_low = split16(stats[2 * heads : 3 * heads])
        gate_term = dot32(
            jnp.concatenate([pre_high, pre_low, pre_high], axis=0),
            jnp.concatenate([weight_high, weight_high, weight_low], axis=0),
            TN,
        )
        key_acc = jnp.zeros((count * length, head_dim), jnp.float32)
        value_acc = jnp.zeros((count * length, head_dim), jnp.float32)
        for h in range(0, heads, 2):
            first = slice(h * head_dim, (h + 1) * head_dim)
            second = slice((h + 1) * head_dim, (h + 2) * head_dim)
            query_p = jnp.concatenate([query[:, first], query[:, second]], axis=0)
            grad_p = jnp.concatenate([grad[:, first], grad[:, second]], axis=0)
            norm_p = jnp.concatenate([stats[h : h + 1], stats[h + 1 : h + 2]], axis=1)
            inner_p = jnp.concatenate(
                [stats[heads + h : heads + h + 1], stats[heads + h + 1 : heads + h + 2]], axis=1
            )
            scores = dot32(keys, query_p, NT)
            raw = dot32(values, grad_p, NT)
            probs = jnp.exp2(scores * (factor * LOG2E) - (masked + norm_p))
            dscores = (probs * (raw - inner_p)).astype(jnp.bfloat16)
            value_acc += dot32(probs.astype(jnp.bfloat16), grad_p)
            key_acc += dot32(dscores, query_p)
            turned = dot32(keys_t, dscores).T
            query_grad[:, first] = (factor * turned[:length] + gate_term[:, first]).astype(
                jnp.bfloat16
            )
            query_grad[:, second] = (factor * turned[length:] + gate_term[:, second]).astype(
                jnp.bfloat16
            )
        for d, ref in enumerate(kv_grad):
            rows = slice(d * length, (d + 1) * length)
            ref[:length] = (factor * key_acc[rows]).astype(jnp.bfloat16)
            ref[length:] = value_acc[rows].astype(jnp.bfloat16)


def up_route(sections, size, d):
    route = {}
    for r in range(size):
        for s in range(2, sections):
            route[s, r] = (s, (r + d) % size)
        if sections > 1:
            route[1, r] = (1, r + d) if r + d < size else (0, r)
        if sections > 1:
            route[0, r] = (0, r - d) if r >= d else (1, r)
        else:
            route[0, r] = (0, r)
    return [(s * size + r, t * size + q) for (s, r), (t, q) in sorted(route.items())]


def down_route(sections, size, d):
    route = {}
    for r in range(size):
        for s in range(1, sections):
            if r >= d:
                route[s, r] = (s - 1, r - d)
    taken = set(route.values())
    if sections == 2 and d:
        for a in range(size - d):
            if a == size - 1 - d:
                for u in range(a, size - 1):
                    route[0, u] = (0, u + 1)
                route[0, size - 1] = (1, size - 1)
            elif a < d:
                route[0, a] = (1, a)
                route[1, a] = (1, a + d)
            else:
                route[0, a] = (1, a + d)
        for r in range(size):
            for s in range(2):
                route.setdefault((s, r), (s, r))
    else:
        free = [(s, r) for s in range(sections) for r in range(size) if (s, r) not in route]
        ends = [(s, r) for s in range(sections) for r in range(size) if (s, r) not in taken]
        route.update(zip(free, ends[-len(free) :], strict=True))
    return [(s * size + r, t * size + q) for (s, r), (t, q) in sorted(route.items())]


def shifted(array, axis):
    size = lax.axis_size(axis)
    return [
        lax.ppermute(array, axis, [(i, (i + d) % size) for i in range(size)])
        for d in range(1, size)
    ]


def on_device(
    queries, key_rows, value_rows, out_grad, attn_out, log_norm, selected, gate_weight, gate_bias
):
    length, width = queries.shape[2:]
    _, heads, head_dim = gate_weight.shape
    size = lax.axis_size("ctx")
    sections = lax.axis_size("section")
    local = length // BLK
    both_axes = ("section", "ctx")
    dma = pltpu.SemaphoreType.DMA
    hbm = pl.BlockSpec(memory_space=pltpu.HBM)
    vmem = pl.BlockSpec(memory_space=pltpu.VMEM)
    params = pltpu.CompilerParams(vmem_limit_bytes=VMEM_BYTES)

    def in_hbm(array):
        return pltpu.with_memory_space_constraint(array, pltpu.HBM)

    def shape(*dims, dtype=jnp.float32):
        return jax.ShapeDtypeStruct(dims, dtype)

    own_kv = pl.pallas_call(
        pack_kernel,
        out_shape=shape(2 * length, head_dim, dtype=jnp.bfloat16),
        in_specs=[hbm, hbm],
        out_specs=vmem,
        scratch_shapes=[dma((2,))],
        compiler_params=params,
        name="pack_keys_values",
    )(in_hbm(key_rows[0, 0]), in_hbm(value_rows[0, 0]))
    kv = [own_kv]
    for d in range(1, size):
        kv.append(lax.ppermute(own_kv, both_axes, up_route(sections, size, d)))
    query, grad, weight, stats, partial = pl.pallas_call(
        functools.partial(stats_kernel, size),
        out_shape=(
            shape(length, width, dtype=jnp.bfloat16),
            shape(length, width, dtype=jnp.bfloat16),
            shape(heads, head_dim),
            shape(3 * heads + size * local, length),
            shape(heads + 8, head_dim),
        ),
        in_specs=[hbm] * 7,
        out_specs=(vmem,) * 5,
        scratch_shapes=[
            pltpu.VMEM((length, width), jnp.bfloat16),
            pltpu.VMEM((heads, length), jnp.float32),
            pltpu.VMEM((1, heads), jnp.float32),
            pltpu.VMEM(selected.shape[2:], jnp.int32),
            dma((7,)),
        ],
        compiler_params=params,
        cost_estimate=pl.CostEstimate(
            flops=8 * heads * length * width, transcendentals=0, bytes_accessed=6 * length * width
        ),
        name="gate_stats",
    )(
        *map(
            in_hbm,
            (
                gate_weight[0],
                log_norm[0, 0].T,
                gate_bias,
                selected[0, 0],
                queries[0, 0],
                out_grad[0, 0],
                attn_out[0, 0],
            ),
        )
    )
    partial, *kv = lax.optimization_barrier((partial, *kv))
    by_dp = shifted(partial, "dp")
    results = pl.pallas_call(
        functools.partial(attention_kernel, size),
        out_shape=(shape(length, width, dtype=jnp.bfloat16),)
        + (shape(2 * length, head_dim, dtype=jnp.bfloat16),) * size,
        compiler_params=params,
        cost_estimate=pl.CostEstimate(
            flops=10 * size * length * length * width,
            transcendentals=size * length * length * heads,
            bytes_accessed=6 * length * width,
        ),
        name="attention_grads",
    )(query, grad, stats, weight, *kv)
    *results, partial = lax.optimization_barrier(
        (*results, functools.reduce(jnp.add, by_dp, partial))
    )
    query_sent = lax.ppermute(
        results[0], "section", [(s, (s - 1) % sections) for s in range(sections)]
    )
    kv_parts = [
        lax.ppermute(part, both_axes, down_route(sections, size, d))
        for d, part in enumerate(results[1:])
    ]
    parts = [partial] + shifted(partial, "ctx")
    key_grad, value_grad, weight_grad, bias_grad = pl.pallas_call(
        functools.partial(final_kernel, size, len(parts)),
        out_shape=(
            shape(length, head_dim, dtype=jnp.bfloat16),
            shape(length, head_dim, dtype=jnp.bfloat16),
            shape(heads, head_dim),
            shape(1, heads),
        ),
        compiler_params=params,
        name="final_sums",
    )(*kv_parts, *parts)
    return (
        query_sent[None, None],
        key_grad[None, None],
        value_grad[None, None],
        weight_grad[None],
        bias_grad,
    )


def solution(mesh):
    rows = P("dp", "section", "ctx", None)
    return jax.shard_map(
        on_device,
        mesh=mesh,
        in_specs=(rows,) * 7 + (P("section", None, None), P("section", None)),
        out_specs=(rows,) * 3 + (P("section", None, None), P("section", None)),
        check_vma=False,
    )
```

```python
import functools

import jax
import jax.numpy as jnp
from jax import lax
from jax.experimental import pallas as pl
from jax.experimental.pallas import tpu as pltpu
from jax.sharding import PartitionSpec as P

BLK = 64
FINAL_COST = 10000000000
QUERY_COST = 10000000000
OUT = 1e30
LOG2E = 1.4426950408889634
NT = (((1,), (1,)), ((), ()))
TN = (((0,), (0,)), ((), ()))
VMEM_BYTES = 24 * 1024 * 1024


def dot32(a, b, dims=(((1,), (0,)), ((), ())), precision=None):
    return lax.dot_general(a, b, dims, precision=precision, preferred_element_type=jnp.float32)


def split16(x):
    high = x.astype(jnp.bfloat16)
    low = (x - high.astype(jnp.float32)).astype(jnp.bfloat16)
    return high, low


def head_blocks(weight):
    heads = weight.shape[0]
    row = lax.broadcasted_iota(jnp.int32, weight.shape, 0)
    return jnp.concatenate([jnp.where(row == h, weight, 0.0) for h in range(heads)], axis=1)


def load_kernel(*refs):
    keys, values, *sources = refs[:9]
    packed, *targets, sems = refs[9:]
    length = keys.shape[0]
    copies = [
        pltpu.make_async_copy(source, target, sems.at[i])
        for i, (source, target) in enumerate(
            zip(
                (keys, values, *sources),
                (packed.at[:length], packed.at[length:], *targets),
                strict=True,
            )
        )
    ]
    for copy in copies:
        copy.start()
    for copy in copies:
        copy.wait()


def stats_kernel(count, *refs):
    weight, norm, bias, chosen, query, grad, output, stats, partial = refs
    heads, head_dim = weight.shape
    length = query.shape[0]
    local = length // BLK
    rank = lax.axis_index("ctx")
    listed = chosen[...]
    lane_block = lax.broadcasted_iota(jnp.int32, (1, length), 1) // BLK
    for d in range(count):
        for b in range(local):
            block = lax.rem(rank - d + count, count) * local + b
            hit = jnp.max(jnp.where(listed == block, 1.0, 0.0), axis=1, keepdims=True)
            one = jnp.zeros((1, length), jnp.float32)
            for at in range(local):
                one = jnp.where(lane_block == at, (1.0 - hit[at : at + 1]) * OUT, one)
            at = 3 * heads + d * local + b
            stats[at : at + 1] = one
    eye = (
        lax.broadcasted_iota(jnp.int32, (heads, heads), 0)
        == lax.broadcasted_iota(jnp.int32, (heads, heads), 1)
    ).astype(jnp.float32)
    bias_col = jnp.sum(eye * bias[...], axis=1, keepdims=True)
    weight_high, weight_low = split16(head_blocks(weight[...]))
    ones = head_blocks(jnp.ones((heads, head_dim), jnp.float32)).astype(jnp.bfloat16)
    both = dot32(jnp.concatenate([weight_high, weight_low], axis=0), query[...], NT)
    logit = both[:heads] + both[heads:] + bias_col
    gate = jax.nn.sigmoid(logit)
    softplus = jnp.maximum(-logit, 0.0) + jnp.log1p(jnp.exp(-jnp.abs(logit)))
    stats[0:heads] = LOG2E * (norm[...] + softplus)
    product = grad[...].astype(jnp.float32) * output[...].astype(jnp.float32)
    high, low = split16(product)
    inner = dot32(ones, high, NT) + dot32(ones, low, NT)
    pre_grad = inner * gate * (1.0 - gate)
    stats[heads : 2 * heads] = inner
    stats[2 * heads : 3 * heads] = pre_grad
    pre_high, pre_low = split16(pre_grad)
    wide = dot32(jnp.concatenate([pre_high, pre_low], axis=0), query[...])
    wide = wide[:heads] + wide[heads:]
    total = jnp.sum(pre_grad, axis=1, keepdims=True)
    lane = lax.broadcasted_iota(jnp.int32, (heads, head_dim), 1)
    row = lax.broadcasted_iota(jnp.int32, (heads, head_dim), 0)
    bias_row = jnp.sum(jnp.where(lane == row, total, 0.0), axis=0, keepdims=True)
    one = jnp.zeros((heads, head_dim), jnp.float32)
    for h in range(heads):
        one += jnp.where(row == h, wide[:, h * head_dim : (h + 1) * head_dim], 0.0)
    bias_rows = jnp.broadcast_to(bias_row, (8, head_dim))
    for i in range(partial.shape[0]):
        partial[i, :heads] = one
        partial[i, heads:] = bias_rows


def final_kernel(*refs):
    *kv, parts, key_grad, value_grad, weight_grad, bias_grad = refs
    length = key_grad.shape[0]
    heads = weight_grad.shape[0]
    total = jnp.sum(parts[...], axis=0)
    weight_grad[...] = total[:heads]
    bias_grad[...] = total[heads : heads + 1, :heads]
    total = functools.reduce(jnp.add, [ref[...].astype(jnp.float32) for ref in kv])
    total = total.astype(jnp.bfloat16)
    key_grad[...] = total[:length]
    value_grad[...] = total[length:]


def scores_kernel(count, *refs):
    query, grad, stats = refs[:3]
    kv = refs[3 : 3 + count]
    dscores_out = refs[3 + count]
    kv_grad = refs[4 + count :]
    length = query.shape[0]
    head_dim = kv[0].shape[1]
    heads = query.shape[1] // head_dim
    local = length // BLK
    factor = head_dim ** (-0.5)
    section = lax.axis_index("section")

    @pl.when(section == 0)
    def _():
        for ref in kv_grad:
            ref[...] = jnp.zeros_like(ref)

    @pl.when(section > 0)
    def _():
        keys = jnp.concatenate([ref[:length] for ref in kv], axis=0)
        values = jnp.concatenate([ref[length:] for ref in kv], axis=0)
        outs = [
            jnp.broadcast_to(stats[3 * heads + i : 3 * heads + i + 1], (BLK, length))
            for i in range(count * local)
        ]
        later = lax.broadcasted_iota(jnp.int32, (length, length), 0) > lax.broadcasted_iota(
            jnp.int32, (length, length), 1
        )
        own = jnp.where(later, OUT, jnp.concatenate(outs[:local], axis=0))
        masked = jnp.concatenate([own] + outs[local:], axis=0)
        masked = jnp.concatenate([masked, masked], axis=1)
        key_acc = jnp.zeros((count * length, head_dim), jnp.float32)
        value_acc = jnp.zeros((count * length, head_dim), jnp.float32)
        for h in range(0, heads, 2):
            first = slice(h * head_dim, (h + 1) * head_dim)
            second = slice((h + 1) * head_dim, (h + 2) * head_dim)
            query_p = jnp.concatenate([query[:, first], query[:, second]], axis=0)
            grad_p = jnp.concatenate([grad[:, first], grad[:, second]], axis=0)
            norm_p = jnp.concatenate([stats[h : h + 1], stats[h + 1 : h + 2]], axis=1)
            inner_p = jnp.concatenate(
                [stats[heads + h : heads + h + 1], stats[heads + h + 1 : heads + h + 2]], axis=1
            )
            scores = dot32(keys, query_p, NT)
            raw = dot32(values, grad_p, NT)
            probs = jnp.exp2(scores * (factor * LOG2E) - (masked + norm_p))
            dscores = (probs * (raw - inner_p)).astype(jnp.bfloat16)
            value_acc += dot32(probs.astype(jnp.bfloat16), grad_p)
            key_acc += dot32(dscores, query_p)
            dscores_out[:, h * length : (h + 2) * length] = dscores
        for d, ref in enumerate(kv_grad):
            rows = slice(d * length, (d + 1) * length)
            ref[:length] = (factor * key_acc[rows]).astype(jnp.bfloat16)
            ref[length:] = value_acc[rows].astype(jnp.bfloat16)


def query_kernel(count, *refs):
    dscores, stats, weight = refs[:3]
    kv = refs[3 : 3 + count]
    packed = refs[3 + count]
    heads, head_dim = weight.shape
    length = packed.shape[0]
    factor = head_dim ** (-0.5)
    section = lax.axis_index("section")

    @pl.when(section == 0)
    def _():
        packed[...] = jnp.zeros_like(packed)

    @pl.when(section > 0)
    def _():
        keys_t = jnp.concatenate([ref[:length] for ref in kv], axis=0).T
        weight_high, weight_low = split16(head_blocks(weight[...]))
        pre_high, pre_low = split16(stats[2 * heads : 3 * heads])
        gate_term = dot32(
            jnp.concatenate([pre_high, pre_low, pre_high], axis=0),
            jnp.concatenate([weight_high, weight_high, weight_low], axis=0),
            TN,
        )
        for h in range(0, heads, 2):
            turned = dot32(keys_t, dscores[:, h * length : (h + 2) * length]).T
            for at in range(2):
                columns = slice((h + at) * head_dim, (h + at + 1) * head_dim)
                packed[:, columns] = (
                    factor * turned[at * length : (at + 1) * length] + gate_term[:, columns]
                ).astype(jnp.bfloat16)


def up_route(sections, size, d):
    route = {}
    for r in range(size):
        for s in range(2, sections):
            route[s, r] = (s, (r + d) % size)
        if sections > 1:
            route[1, r] = (1, r + d) if r + d < size else (0, r)
        if sections > 1:
            route[0, r] = (0, r - d) if r >= d else (1, r)
        else:
            route[0, r] = (0, r)
    return [(s * size + r, t * size + q) for (s, r), (t, q) in sorted(route.items())]


def down_route(sections, size, d):
    route = [
        (s * size + r, (s - 1) * size + r - d) for s in range(1, sections) for r in range(d, size)
    ]
    if d == 0:
        route += [(r, (sections - 1) * size + r) for r in range(size)]
    return route


def on_device(
    queries, key_rows, value_rows, out_grad, attn_out, log_norm, selected, gate_weight, gate_bias
):
    length, width = queries.shape[2:]
    _, heads, head_dim = gate_weight.shape
    size = lax.axis_size("ctx")
    sections = lax.axis_size("section")
    local = length // BLK
    both_axes = ("section", "ctx")
    dma = pltpu.SemaphoreType.DMA
    hbm = pl.BlockSpec(memory_space=pltpu.HBM)
    vmem = pl.BlockSpec(memory_space=pltpu.VMEM)
    params = pltpu.CompilerParams(vmem_limit_bytes=VMEM_BYTES)

    def in_hbm(array):
        return pltpu.with_memory_space_constraint(array, pltpu.HBM)

    def shape(*dims, dtype=jnp.float32):
        return jax.ShapeDtypeStruct(dims, dtype)

    sources = (
        gate_weight[0],
        log_norm[0, 0].T,
        gate_bias,
        selected[0, 0],
        queries[0, 0],
        out_grad[0, 0],
        attn_out[0, 0],
    )
    own_kv, *loaded = pl.pallas_call(
        load_kernel,
        out_shape=(shape(2 * length, head_dim, dtype=jnp.bfloat16),)
        + tuple(shape(*source.shape, dtype=source.dtype) for source in sources),
        in_specs=[hbm] * 9,
        out_specs=(vmem,) * 8,
        scratch_shapes=[dma((9,))],
        compiler_params=params,
        name="load",
    )(*map(in_hbm, (key_rows[0, 0], value_rows[0, 0], *sources)))
    weight, query, grad = loaded[0], loaded[4], loaded[5]
    kv = [own_kv]
    for d in range(1, size):
        kv.append(lax.ppermute(own_kv, both_axes, up_route(sections, size, d)))
    stats, partial = pl.pallas_call(
        functools.partial(stats_kernel, size),
        out_shape=(
            shape(3 * heads + size * local, length),
            shape(size * lax.axis_size("dp"), heads + 8, head_dim),
        ),
        compiler_params=params,
        cost_estimate=pl.CostEstimate(
            flops=8 * heads * length * width, transcendentals=0, bytes_accessed=6 * length * width
        ),
        name="gate_stats",
    )(*loaded)
    partial, kv[1:2] = lax.optimization_barrier((partial, kv[1:2]))
    partial = lax.all_to_all(partial, ("dp", "ctx"), 0, 0)
    dscores, *kv_grad = pl.pallas_call(
        functools.partial(scores_kernel, size),
        out_shape=(shape(size * length, heads * length, dtype=jnp.bfloat16),)
        + (shape(2 * length, head_dim, dtype=jnp.bfloat16),) * size,
        compiler_params=params,
        cost_estimate=pl.CostEstimate(
            flops=8 * size * length * length * width,
            transcendentals=size * length * length * heads,
            bytes_accessed=6 * length * width,
        ),
        name="score_grads",
    )(query, grad, stats, *kv)
    kv_parts = [
        lax.ppermute(kv_grad[d], both_axes, down_route(sections, size, d)) for d in range(size)
    ]
    packed = pl.pallas_call(
        functools.partial(query_kernel, size),
        out_shape=shape(length, width, dtype=jnp.bfloat16),
        compiler_params=params,
        cost_estimate=pl.CostEstimate(
            flops=QUERY_COST,
            transcendentals=0,
            bytes_accessed=6 * length * width,
        ),
        name="query_grads",
    )(dscores, stats, weight, *kv)
    query_sent = lax.ppermute(
        packed, "section", [(s, (s - 1) % sections) for s in range(sections)]
    )
    key_grad, value_grad, weight_grad, bias_grad = pl.pallas_call(
        final_kernel,
        out_shape=(
            shape(length, head_dim, dtype=jnp.bfloat16),
            shape(length, head_dim, dtype=jnp.bfloat16),
            shape(heads, head_dim),
            shape(1, heads),
        ),
        compiler_params=params,
        cost_estimate=pl.CostEstimate(
            flops=FINAL_COST, transcendentals=0, bytes_accessed=4 * length * width
        ),
        name="final_sums",
    )(*kv_parts[::-1], partial)
    return (
        query_sent[None, None],
        key_grad[None, None],
        value_grad[None, None],
        weight_grad[None],
        bias_grad,
    )


def solution(mesh):
    rows = P("dp", "section", "ctx", None)
    return jax.shard_map(
        on_device,
        mesh=mesh,
        in_specs=(rows,) * 7 + (P("section", None, None), P("section", None)),
        out_specs=(rows,) * 3 + (P("section", None, None), P("section", None)),
        check_vma=False,
    )
```

```python
import functools

import jax
import jax.numpy as jnp
from jax import lax
from jax.experimental import pallas as pl
from jax.experimental.pallas import tpu as pltpu
from jax.sharding import PartitionSpec as P

BLK = 64
FINAL_COST = 10000000000
QUERY_COST = 10000000000
OUT = 1e30
LOG2E = 1.4426950408889634
NT = (((1,), (1,)), ((), ()))
TN = (((0,), (0,)), ((), ()))
VMEM_BYTES = 24 * 1024 * 1024


def dot32(a, b, dims=(((1,), (0,)), ((), ())), precision=None):
    return lax.dot_general(a, b, dims, precision=precision, preferred_element_type=jnp.float32)


def split16(x):
    high = x.astype(jnp.bfloat16)
    low = (x - high.astype(jnp.float32)).astype(jnp.bfloat16)
    return high, low


def head_blocks(weight):
    heads = weight.shape[0]
    row = lax.broadcasted_iota(jnp.int32, weight.shape, 0)
    return jnp.concatenate([jnp.where(row == h, weight, 0.0) for h in range(heads)], axis=1)


def load_kernel(*refs):
    keys, values, *sources = refs[:9]
    packed, *targets, sems = refs[9:]
    length = keys.shape[0]
    copies = [
        pltpu.make_async_copy(source, target, sems.at[i])
        for i, (source, target) in enumerate(
            zip(
                (keys, values, *sources),
                (packed.at[:length], packed.at[length:], *targets),
                strict=True,
            )
        )
    ]
    for copy in copies:
        copy.start()
    for copy in copies:
        copy.wait()


def stats_kernel(count, *refs):
    weight, norm, bias, chosen, query, grad, output, stats, partial = refs
    heads, head_dim = weight.shape
    length = query.shape[0]
    local = length // BLK
    rank = lax.axis_index("ctx")
    listed = chosen[...]
    lane_block = lax.broadcasted_iota(jnp.int32, (1, length), 1) // BLK
    for d in range(count):
        for b in range(local):
            block = lax.rem(rank - d + count, count) * local + b
            hit = jnp.max(jnp.where(listed == block, 1.0, 0.0), axis=1, keepdims=True)
            one = jnp.zeros((1, length), jnp.float32)
            for at in range(local):
                one = jnp.where(lane_block == at, (1.0 - hit[at : at + 1]) * OUT, one)
            at = 3 * heads + d * local + b
            stats[at : at + 1] = one
    eye = (
        lax.broadcasted_iota(jnp.int32, (heads, heads), 0)
        == lax.broadcasted_iota(jnp.int32, (heads, heads), 1)
    ).astype(jnp.float32)
    bias_col = jnp.sum(eye * bias[...], axis=1, keepdims=True)
    weight_high, weight_low = split16(head_blocks(weight[...]))
    ones = head_blocks(jnp.ones((heads, head_dim), jnp.float32)).astype(jnp.bfloat16)
    both = dot32(jnp.concatenate([weight_high, weight_low], axis=0), query[...], NT)
    logit = both[:heads] + both[heads:] + bias_col
    gate = jax.nn.sigmoid(logit)
    softplus = jnp.maximum(-logit, 0.0) + jnp.log1p(jnp.exp(-jnp.abs(logit)))
    stats[0:heads] = LOG2E * (norm[...] + softplus)
    product = grad[...].astype(jnp.float32) * output[...].astype(jnp.float32)
    high, low = split16(product)
    inner = dot32(ones, high, NT) + dot32(ones, low, NT)
    pre_grad = inner * gate * (1.0 - gate)
    stats[heads : 2 * heads] = inner
    stats[2 * heads : 3 * heads] = pre_grad
    pre_high, pre_low = split16(pre_grad)
    wide = dot32(jnp.concatenate([pre_high, pre_low], axis=0), query[...])
    wide = wide[:heads] + wide[heads:]
    total = jnp.sum(pre_grad, axis=1, keepdims=True)
    lane = lax.broadcasted_iota(jnp.int32, (heads, head_dim), 1)
    row = lax.broadcasted_iota(jnp.int32, (heads, head_dim), 0)
    bias_row = jnp.sum(jnp.where(lane == row, total, 0.0), axis=0, keepdims=True)
    one = jnp.zeros((heads, head_dim), jnp.float32)
    for h in range(heads):
        one += jnp.where(row == h, wide[:, h * head_dim : (h + 1) * head_dim], 0.0)
    bias_rows = jnp.broadcast_to(bias_row, (8, head_dim))
    for i in range(partial.shape[0]):
        partial[i, :heads] = one
        partial[i, heads:] = bias_rows


def final_kernel(*refs):
    *kv, parts, kv_total, gate_total = refs
    gate_total[...] = jnp.sum(parts[...], axis=0)
    total = functools.reduce(jnp.add, [ref[...].astype(jnp.float32) for ref in kv])
    kv_total[...] = total.astype(jnp.bfloat16)


def output_kernel(query, kv_total, gate_total, *refs):
    query_grad, key_grad, value_grad, weight_grad, bias_grad, bias, sems = refs
    length = key_grad.shape[0]
    heads = weight_grad.shape[0]
    copies = [
        pltpu.make_async_copy(source, target, sems.at[i])
        for i, (source, target) in enumerate(
            (
                (query.at[: length // 2], query_grad.at[: length // 2]),
                (query.at[length // 2 :], query_grad.at[length // 2 :]),
                (kv_total.at[:length], key_grad),
                (kv_total.at[length:], value_grad),
                (gate_total.at[:heads], weight_grad),
                (bias, bias_grad),
            )
        )
    ]
    for copy in copies[:-1]:
        copy.start()
    bias[...] = gate_total[heads : heads + 1, :heads]
    copies[-1].start()
    for copy in copies:
        copy.wait()


def scores_kernel(count, *refs):
    query, grad, stats = refs[:3]
    kv = refs[3 : 3 + count]
    dscores_out = refs[3 + count]
    kv_grad = refs[4 + count :]
    length = query.shape[0]
    head_dim = kv[0].shape[1]
    heads = query.shape[1] // head_dim
    local = length // BLK
    factor = head_dim ** (-0.5)
    section = lax.axis_index("section")

    @pl.when(section == 0)
    def _():
        for ref in kv_grad:
            ref[...] = jnp.zeros_like(ref)

    @pl.when(section > 0)
    def _():
        keys = jnp.concatenate([ref[:length] for ref in kv], axis=0)
        values = jnp.concatenate([ref[length:] for ref in kv], axis=0)
        outs = [
            jnp.broadcast_to(stats[3 * heads + i : 3 * heads + i + 1], (BLK, length))
            for i in range(count * local)
        ]
        later = lax.broadcasted_iota(jnp.int32, (length, length), 0) > lax.broadcasted_iota(
            jnp.int32, (length, length), 1
        )
        own = jnp.where(later, OUT, jnp.concatenate(outs[:local], axis=0))
        masked = jnp.concatenate([own] + outs[local:], axis=0)
        masked = jnp.concatenate([masked, masked], axis=1)
        key_acc = jnp.zeros((count * length, head_dim), jnp.float32)
        value_acc = jnp.zeros((count * length, head_dim), jnp.float32)
        for h in range(0, heads, 2):
            first = slice(h * head_dim, (h + 1) * head_dim)
            second = slice((h + 1) * head_dim, (h + 2) * head_dim)
            query_p = jnp.concatenate([query[:, first], query[:, second]], axis=0)
            grad_p = jnp.concatenate([grad[:, first], grad[:, second]], axis=0)
            norm_p = jnp.concatenate([stats[h : h + 1], stats[h + 1 : h + 2]], axis=1)
            inner_p = jnp.concatenate(
                [stats[heads + h : heads + h + 1], stats[heads + h + 1 : heads + h + 2]], axis=1
            )
            scores = dot32(keys, query_p, NT)
            raw = dot32(values, grad_p, NT)
            probs = jnp.exp2(scores * (factor * LOG2E) - (masked + norm_p))
            dscores = (probs * (raw - inner_p)).astype(jnp.bfloat16)
            value_acc += dot32(probs.astype(jnp.bfloat16), grad_p)
            key_acc += dot32(dscores, query_p)
            dscores_out[:, h * length : (h + 2) * length] = dscores
        for d, ref in enumerate(kv_grad):
            rows = slice(d * length, (d + 1) * length)
            ref[:length] = (factor * key_acc[rows]).astype(jnp.bfloat16)
            ref[length:] = value_acc[rows].astype(jnp.bfloat16)


def query_kernel(count, *refs):
    dscores, stats, weight = refs[:3]
    kv = refs[3 : 3 + count]
    packed = refs[3 + count]
    heads, head_dim = weight.shape
    length = packed.shape[0]
    factor = head_dim ** (-0.5)
    section = lax.axis_index("section")

    @pl.when(section == 0)
    def _():
        packed[...] = jnp.zeros_like(packed)

    @pl.when(section > 0)
    def _():
        keys_t = jnp.concatenate([ref[:length] for ref in kv], axis=0).T
        weight_high, weight_low = split16(head_blocks(weight[...]))
        pre_high, pre_low = split16(stats[2 * heads : 3 * heads])
        gate_term = dot32(
            jnp.concatenate([pre_high, pre_low, pre_high], axis=0),
            jnp.concatenate([weight_high, weight_high, weight_low], axis=0),
            TN,
        )
        for h in range(0, heads, 2):
            turned = dot32(keys_t, dscores[:, h * length : (h + 2) * length]).T
            for at in range(2):
                columns = slice((h + at) * head_dim, (h + at + 1) * head_dim)
                packed[:, columns] = (
                    factor * turned[at * length : (at + 1) * length] + gate_term[:, columns]
                ).astype(jnp.bfloat16)


def up_route(sections, size, d):
    route = {}
    for r in range(size):
        for s in range(2, sections):
            route[s, r] = (s, (r + d) % size)
        if sections > 1:
            route[1, r] = (1, r + d) if r + d < size else (0, r)
        if sections > 1:
            route[0, r] = (0, r - d) if r >= d else (1, r)
        else:
            route[0, r] = (0, r)
    return [(s * size + r, t * size + q) for (s, r), (t, q) in sorted(route.items())]


def down_route(sections, size, d):
    route = [
        (s * size + r, (s - 1) * size + r - d) for s in range(1, sections) for r in range(d, size)
    ]
    if d == 0:
        route += [(r, (sections - 1) * size + r) for r in range(size)]
    return route


def on_device(
    queries, key_rows, value_rows, out_grad, attn_out, log_norm, selected, gate_weight, gate_bias
):
    length, width = queries.shape[2:]
    _, heads, head_dim = gate_weight.shape
    size = lax.axis_size("ctx")
    sections = lax.axis_size("section")
    local = length // BLK
    both_axes = ("section", "ctx")
    dma = pltpu.SemaphoreType.DMA
    hbm = pl.BlockSpec(memory_space=pltpu.HBM)
    vmem = pl.BlockSpec(memory_space=pltpu.VMEM)
    params = pltpu.CompilerParams(vmem_limit_bytes=VMEM_BYTES)

    def in_hbm(array):
        return pltpu.with_memory_space_constraint(array, pltpu.HBM)

    def shape(*dims, dtype=jnp.float32):
        return jax.ShapeDtypeStruct(dims, dtype)

    sources = (
        gate_weight[0],
        log_norm[0, 0].T,
        gate_bias,
        selected[0, 0],
        queries[0, 0],
        out_grad[0, 0],
        attn_out[0, 0],
    )
    own_kv, *loaded = pl.pallas_call(
        load_kernel,
        out_shape=(shape(2 * length, head_dim, dtype=jnp.bfloat16),)
        + tuple(shape(*source.shape, dtype=source.dtype) for source in sources),
        in_specs=[hbm] * 9,
        out_specs=(vmem,) * 8,
        scratch_shapes=[dma((9,))],
        compiler_params=params,
        name="load",
    )(*map(in_hbm, (key_rows[0, 0], value_rows[0, 0], *sources)))
    weight, query, grad = loaded[0], loaded[4], loaded[5]
    kv = [own_kv]
    for d in range(1, size):
        kv.append(lax.ppermute(own_kv, both_axes, up_route(sections, size, d)))
    stats, partial = pl.pallas_call(
        functools.partial(stats_kernel, size),
        out_shape=(
            shape(3 * heads + size * local, length),
            shape(size * lax.axis_size("dp"), heads + 8, head_dim),
        ),
        compiler_params=params,
        cost_estimate=pl.CostEstimate(
            flops=8 * heads * length * width, transcendentals=0, bytes_accessed=6 * length * width
        ),
        name="gate_stats",
    )(*loaded)
    partial = lax.all_to_all(partial, ("dp", "ctx"), 0, 0)
    dscores, *kv_grad = pl.pallas_call(
        functools.partial(scores_kernel, size),
        out_shape=(shape(size * length, heads * length, dtype=jnp.bfloat16),)
        + (shape(2 * length, head_dim, dtype=jnp.bfloat16),) * size,
        compiler_params=params,
        cost_estimate=pl.CostEstimate(
            flops=8 * size * length * length * width,
            transcendentals=size * length * length * heads,
            bytes_accessed=6 * length * width,
        ),
        name="score_grads",
    )(query, grad, stats, *kv)
    kv_parts = [
        lax.ppermute(kv_grad[d], both_axes, down_route(sections, size, d)) for d in range(size)
    ]
    packed = pl.pallas_call(
        functools.partial(query_kernel, size),
        out_shape=shape(length, width, dtype=jnp.bfloat16),
        compiler_params=params,
        cost_estimate=pl.CostEstimate(
            flops=QUERY_COST,
            transcendentals=0,
            bytes_accessed=6 * length * width,
        ),
        name="query_grads",
    )(dscores, stats, weight, *kv)
    query_sent = lax.ppermute(
        packed, "section", [(s, (s - 1) % sections) for s in range(sections)]
    )
    kv_total, gate_total = pl.pallas_call(
        final_kernel,
        out_shape=(
            shape(2 * length, head_dim, dtype=jnp.bfloat16),
            shape(heads + 8, head_dim),
        ),
        compiler_params=params,
        cost_estimate=pl.CostEstimate(
            flops=FINAL_COST, transcendentals=0, bytes_accessed=4 * length * width
        ),
        name="final_sums",
    )(*kv_parts[::-1], partial)
    query_grad, key_grad, value_grad, weight_grad, bias_grad = pl.pallas_call(
        output_kernel,
        out_shape=(
            shape(length, width, dtype=jnp.bfloat16),
            shape(length, head_dim, dtype=jnp.bfloat16),
            shape(length, head_dim, dtype=jnp.bfloat16),
            shape(heads, head_dim),
            shape(1, heads),
        ),
        out_specs=(hbm,) * 5,
        scratch_shapes=[pltpu.VMEM((1, heads), jnp.float32), dma((6,))],
        compiler_params=params,
        name="outputs",
    )(query_sent, kv_total, gate_total)
    return (
        query_grad[None, None],
        key_grad[None, None],
        value_grad[None, None],
        weight_grad[None],
        bias_grad,
    )


def solution(mesh):
    rows = P("dp", "section", "ctx", None)
    return jax.shard_map(
        on_device,
        mesh=mesh,
        in_specs=(rows,) * 7 + (P("section", None, None), P("section", None)),
        out_specs=(rows,) * 3 + (P("section", None, None), P("section", None)),
        check_vma=False,
    )
```

```python
import functools

import jax
import jax.numpy as jnp
from jax import lax
from jax.experimental import pallas as pl
from jax.experimental.pallas import tpu as pltpu
from jax.sharding import PartitionSpec as P

BLK = 64
FINAL_COST = 10000000000
QUERY_COST = 10000000000
OUT = 1e30
LOG2E = 1.4426950408889634
NT = (((1,), (1,)), ((), ()))
TN = (((0,), (0,)), ((), ()))
VMEM_BYTES = 24 * 1024 * 1024


def dot32(a, b, dims=(((1,), (0,)), ((), ())), precision=None):
    return lax.dot_general(a, b, dims, precision=precision, preferred_element_type=jnp.float32)


def split16(x):
    high = x.astype(jnp.bfloat16)
    low = (x - high.astype(jnp.float32)).astype(jnp.bfloat16)
    return high, low


def head_blocks(weight):
    heads = weight.shape[0]
    row = lax.broadcasted_iota(jnp.int32, weight.shape, 0)
    return jnp.concatenate([jnp.where(row == h, weight, 0.0) for h in range(heads)], axis=1)


def prepare_kernel(count, *refs):
    sources = refs[:9]
    packed, weight, query, grad, stats, partial = refs[9:15]
    norm, bias, chosen, output, sems = refs[15:]
    heads, head_dim = weight.shape
    length = query.shape[0]
    local = length // BLK
    targets = (
        weight,
        norm,
        bias,
        chosen,
        query,
        grad,
        output,
        packed.at[:length],
        packed.at[length:],
    )
    copies = [
        pltpu.make_async_copy(source, target, sems.at[i])
        for i, (source, target) in enumerate(zip(sources, targets, strict=True))
    ]
    for copy in copies:
        copy.start()
    for copy in copies[:4]:
        copy.wait()
    rank = lax.axis_index("ctx")
    listed = chosen[...]
    lane_block = lax.broadcasted_iota(jnp.int32, (1, length), 1) // BLK
    for d in range(count):
        for b in range(local):
            block = lax.rem(rank - d + count, count) * local + b
            hit = jnp.max(jnp.where(listed == block, 1.0, 0.0), axis=1, keepdims=True)
            one = jnp.zeros((1, length), jnp.float32)
            for at in range(local):
                one = jnp.where(lane_block == at, (1.0 - hit[at : at + 1]) * OUT, one)
            at = 3 * heads + d * local + b
            stats[at : at + 1] = one
    eye = (
        lax.broadcasted_iota(jnp.int32, (heads, heads), 0)
        == lax.broadcasted_iota(jnp.int32, (heads, heads), 1)
    ).astype(jnp.float32)
    bias_col = jnp.sum(eye * bias[...], axis=1, keepdims=True)
    weight_high, weight_low = split16(head_blocks(weight[...]))
    width = heads * head_dim
    indicator = (
        lax.broadcasted_iota(jnp.int32, (width, heads), 0) // head_dim
        == lax.broadcasted_iota(jnp.int32, (width, heads), 1)
    ).astype(jnp.bfloat16)
    copies[4].wait()
    both = dot32(jnp.concatenate([weight_high, weight_low], axis=0), query[...], NT)
    logit = both[:heads] + both[heads:] + bias_col
    gate = jax.nn.sigmoid(logit)
    softplus = jnp.maximum(-logit, 0.0) + jnp.log1p(jnp.exp(-jnp.abs(logit)))
    stats[0:heads] = LOG2E * (norm[...] + softplus)
    slope = gate * (1.0 - gate)
    copies[5].wait()
    copies[6].wait()
    product = grad[...].astype(jnp.float32) * output[...].astype(jnp.float32)
    high, low = split16(product)
    sums = dot32(jnp.concatenate([high, low], axis=0), indicator)
    inner = (sums[:length] + sums[length:]).T
    pre_grad = inner * slope
    stats[heads : 2 * heads] = inner
    stats[2 * heads : 3 * heads] = pre_grad
    pre_high, pre_low = split16(pre_grad)
    wide = dot32(jnp.concatenate([pre_high, pre_low], axis=0), query[...])
    wide = wide[:heads] + wide[heads:]
    total = jnp.sum(pre_grad, axis=1, keepdims=True)
    lane = lax.broadcasted_iota(jnp.int32, (heads, head_dim), 1)
    row = lax.broadcasted_iota(jnp.int32, (heads, head_dim), 0)
    bias_row = jnp.sum(jnp.where(lane == row, total, 0.0), axis=0, keepdims=True)
    one = jnp.zeros((heads, head_dim), jnp.float32)
    for h in range(heads):
        one += jnp.where(row == h, wide[:, h * head_dim : (h + 1) * head_dim], 0.0)
    bias_rows = jnp.broadcast_to(bias_row, (8, head_dim))
    for i in range(partial.shape[0]):
        partial[i, :heads] = one
        partial[i, heads:] = bias_rows
    for copy in copies[7:]:
        copy.wait()


def final_kernel(*refs):
    *kv, parts, kv_total, gate_total = refs
    gate_total[...] = jnp.sum(parts[...], axis=0)
    total = functools.reduce(jnp.add, [ref[...].astype(jnp.float32) for ref in kv])
    kv_total[...] = total.astype(jnp.bfloat16)


def output_kernel(query, kv_total, gate_total, *refs):
    query_grad, key_grad, value_grad, weight_grad, bias_grad, bias, sems = refs
    length = key_grad.shape[0]
    heads = weight_grad.shape[0]
    copies = [
        pltpu.make_async_copy(source, target, sems.at[i])
        for i, (source, target) in enumerate(
            (
                (query.at[: length // 2], query_grad.at[: length // 2]),
                (query.at[length // 2 :], query_grad.at[length // 2 :]),
                (kv_total.at[:length], key_grad),
                (kv_total.at[length:], value_grad),
                (gate_total.at[:heads], weight_grad),
                (bias, bias_grad),
            )
        )
    ]
    for copy in copies[:-1]:
        copy.start()
    bias[...] = gate_total[heads : heads + 1, :heads]
    copies[-1].start()
    for copy in copies:
        copy.wait()


def scores_kernel(count, *refs):
    query, grad, stats = refs[:3]
    kv = refs[3 : 3 + count]
    dscores_out = refs[3 + count]
    kv_grad = refs[4 + count :]
    length = query.shape[0]
    head_dim = kv[0].shape[1]
    heads = query.shape[1] // head_dim
    local = length // BLK
    factor = head_dim ** (-0.5)
    section = lax.axis_index("section")

    @pl.when(section == 0)
    def _():
        for ref in kv_grad:
            ref[...] = jnp.zeros_like(ref)

    @pl.when(section > 0)
    def _():
        keys = jnp.concatenate([ref[:length] for ref in kv], axis=0)
        values = jnp.concatenate([ref[length:] for ref in kv], axis=0)
        outs = [
            jnp.broadcast_to(stats[3 * heads + i : 3 * heads + i + 1], (BLK, length))
            for i in range(count * local)
        ]
        later = lax.broadcasted_iota(jnp.int32, (length, length), 0) > lax.broadcasted_iota(
            jnp.int32, (length, length), 1
        )
        own = jnp.where(later, OUT, jnp.concatenate(outs[:local], axis=0))
        masked = jnp.concatenate([own] + outs[local:], axis=0)
        masked = jnp.concatenate([masked, masked], axis=1)
        key_acc = jnp.zeros((count * length, head_dim), jnp.float32)
        value_acc = jnp.zeros((count * length, head_dim), jnp.float32)
        for h in range(0, heads, 2):
            first = slice(h * head_dim, (h + 1) * head_dim)
            second = slice((h + 1) * head_dim, (h + 2) * head_dim)
            query_p = jnp.concatenate([query[:, first], query[:, second]], axis=0)
            grad_p = jnp.concatenate([grad[:, first], grad[:, second]], axis=0)
            norm_p = jnp.concatenate([stats[h : h + 1], stats[h + 1 : h + 2]], axis=1)
            inner_p = jnp.concatenate(
                [stats[heads + h : heads + h + 1], stats[heads + h + 1 : heads + h + 2]], axis=1
            )
            scores = dot32(keys, query_p, NT)
            raw = dot32(values, grad_p, NT)
            probs = jnp.exp2(scores * (factor * LOG2E) - (masked + norm_p))
            dscores = (probs * (raw - inner_p)).astype(jnp.bfloat16)
            value_acc += dot32(probs.astype(jnp.bfloat16), grad_p)
            key_acc += dot32(dscores, query_p)
            dscores_out[:, h * length : (h + 2) * length] = dscores
        for d, ref in enumerate(kv_grad):
            rows = slice(d * length, (d + 1) * length)
            ref[:length] = (factor * key_acc[rows]).astype(jnp.bfloat16)
            ref[length:] = value_acc[rows].astype(jnp.bfloat16)


def query_kernel(count, *refs):
    dscores, stats, weight = refs[:3]
    kv = refs[3 : 3 + count]
    packed = refs[3 + count]
    heads, head_dim = weight.shape
    length = packed.shape[0]
    factor = head_dim ** (-0.5)
    section = lax.axis_index("section")

    @pl.when(section == 0)
    def _():
        packed[...] = jnp.zeros_like(packed)

    @pl.when(section > 0)
    def _():
        keys_t = jnp.concatenate([ref[:length] for ref in kv], axis=0).T
        weight_high, weight_low = split16(head_blocks(weight[...]))
        pre_high, pre_low = split16(stats[2 * heads : 3 * heads])
        gate_term = dot32(
            jnp.concatenate([pre_high, pre_low, pre_high], axis=0),
            jnp.concatenate([weight_high, weight_high, weight_low], axis=0),
            TN,
        )
        for h in range(0, heads, 2):
            turned = dot32(keys_t, dscores[:, h * length : (h + 2) * length]).T
            for at in range(2):
                columns = slice((h + at) * head_dim, (h + at + 1) * head_dim)
                packed[:, columns] = (
                    factor * turned[at * length : (at + 1) * length] + gate_term[:, columns]
                ).astype(jnp.bfloat16)


def up_route(sections, size, d):
    route = {}
    for r in range(size):
        for s in range(2, sections):
            route[s, r] = (s, (r + d) % size)
        if sections > 1:
            route[1, r] = (1, r + d) if r + d < size else (0, r)
        if sections > 1:
            route[0, r] = (0, r - d) if r >= d else (1, r)
        else:
            route[0, r] = (0, r)
    return [(s * size + r, t * size + q) for (s, r), (t, q) in sorted(route.items())]


def down_route(sections, size, d):
    route = [
        (s * size + r, (s - 1) * size + r - d) for s in range(1, sections) for r in range(d, size)
    ]
    if d == 0:
        route += [(r, (sections - 1) * size + r) for r in range(size)]
    return route


def on_device(
    queries, key_rows, value_rows, out_grad, attn_out, log_norm, selected, gate_weight, gate_bias
):
    length, width = queries.shape[2:]
    _, heads, head_dim = gate_weight.shape
    size = lax.axis_size("ctx")
    sections = lax.axis_size("section")
    local = length // BLK
    both_axes = ("section", "ctx")
    dma = pltpu.SemaphoreType.DMA
    hbm = pl.BlockSpec(memory_space=pltpu.HBM)
    vmem = pl.BlockSpec(memory_space=pltpu.VMEM)
    params = pltpu.CompilerParams(vmem_limit_bytes=VMEM_BYTES)

    def in_hbm(array):
        return pltpu.with_memory_space_constraint(array, pltpu.HBM)

    def shape(*dims, dtype=jnp.float32):
        return jax.ShapeDtypeStruct(dims, dtype)

    sources = (
        gate_weight[0],
        log_norm[0, 0].T,
        gate_bias,
        selected[0, 0],
        queries[0, 0],
        out_grad[0, 0],
        attn_out[0, 0],
    )
    own_kv, weight, query, grad, stats, partial = pl.pallas_call(
        functools.partial(prepare_kernel, size),
        out_shape=(
            shape(2 * length, head_dim, dtype=jnp.bfloat16),
            shape(heads, head_dim),
            shape(length, width, dtype=jnp.bfloat16),
            shape(length, width, dtype=jnp.bfloat16),
            shape(3 * heads + size * local, length),
            shape(size * lax.axis_size("dp"), heads + 8, head_dim),
        ),
        in_specs=[hbm] * 9,
        out_specs=(vmem,) * 6,
        scratch_shapes=[
            pltpu.VMEM((heads, length), jnp.float32),
            pltpu.VMEM((1, heads), jnp.float32),
            pltpu.VMEM(selected.shape[2:], jnp.int32),
            pltpu.VMEM((length, width), jnp.bfloat16),
            dma((9,)),
        ],
        compiler_params=params,
        cost_estimate=pl.CostEstimate(
            flops=8 * heads * length * width, transcendentals=0, bytes_accessed=6 * length * width
        ),
        name="prepare",
    )(*map(in_hbm, (*sources, key_rows[0, 0], value_rows[0, 0])))
    kv = [own_kv]
    for d in range(1, size):
        kv.append(lax.ppermute(own_kv, both_axes, up_route(sections, size, d)))
    partial = lax.all_to_all(partial, ("dp", "ctx"), 0, 0)
    dscores, *kv_grad = pl.pallas_call(
        functools.partial(scores_kernel, size),
        out_shape=(shape(size * length, heads * length, dtype=jnp.bfloat16),)
        + (shape(2 * length, head_dim, dtype=jnp.bfloat16),) * size,
        compiler_params=params,
        cost_estimate=pl.CostEstimate(
            flops=8 * size * length * length * width,
            transcendentals=size * length * length * heads,
            bytes_accessed=6 * length * width,
        ),
        name="score_grads",
    )(query, grad, stats, *kv)
    kv_parts = [
        lax.ppermute(kv_grad[d], both_axes, down_route(sections, size, d)) for d in range(size)
    ]
    packed = pl.pallas_call(
        functools.partial(query_kernel, size),
        out_shape=shape(length, width, dtype=jnp.bfloat16),
        compiler_params=params,
        cost_estimate=pl.CostEstimate(
            flops=QUERY_COST,
            transcendentals=0,
            bytes_accessed=6 * length * width,
        ),
        name="query_grads",
    )(dscores, stats, weight, *kv)
    query_sent = lax.ppermute(
        packed, "section", [(s, (s - 1) % sections) for s in range(sections)]
    )
    kv_total, gate_total = pl.pallas_call(
        final_kernel,
        out_shape=(
            shape(2 * length, head_dim, dtype=jnp.bfloat16),
            shape(heads + 8, head_dim),
        ),
        compiler_params=params,
        cost_estimate=pl.CostEstimate(
            flops=FINAL_COST, transcendentals=0, bytes_accessed=4 * length * width
        ),
        name="final_sums",
    )(*kv_parts[::-1], partial)
    query_grad, key_grad, value_grad, weight_grad, bias_grad = pl.pallas_call(
        output_kernel,
        out_shape=(
            shape(length, width, dtype=jnp.bfloat16),
            shape(length, head_dim, dtype=jnp.bfloat16),
            shape(length, head_dim, dtype=jnp.bfloat16),
            shape(heads, head_dim),
            shape(1, heads),
        ),
        out_specs=(hbm,) * 5,
        scratch_shapes=[pltpu.VMEM((1, heads), jnp.float32), dma((6,))],
        compiler_params=params,
        name="outputs",
    )(query_sent, kv_total, gate_total)
    return (
        query_grad[None, None],
        key_grad[None, None],
        value_grad[None, None],
        weight_grad[None],
        bias_grad,
    )


def solution(mesh):
    rows = P("dp", "section", "ctx", None)
    return jax.shard_map(
        on_device,
        mesh=mesh,
        in_specs=(rows,) * 7 + (P("section", None, None), P("section", None)),
        out_specs=(rows,) * 3 + (P("section", None, None), P("section", None)),
        check_vma=False,
    )
```
